32 devices in a mesh: expert: 8 (over y, x, core), tensor: 4 (over z).
Axes of the slice: x: 2, y: 2, z: 4, core: 2. Of those that a mesh axis runs over, the one named last changes fastest.
Arguments:
- tokens: bfloat16 [512, 4096], P(('expert', 'tensor')), may hold values from -6 to 6
- grad_out: bfloat16 [512, 4096], P(('expert', 'tensor')), may hold values from -1.5 to 1.5
- routes: int32 [512, 8], P(('expert', 'tensor')), may hold values from 0 to 15, all different within a row; in each aligned block of 16 rows (0 to 15, 16 to 31, ...) at most 12 rows name the same one
- gate_probs: bfloat16 [512, 8], P(('expert', 'tensor')), may hold values from 0.019897461 to 0.29882812
- w_gate: bfloat16 [16, 1536, 4096], P('expert', 'tensor'), may hold values from -0.09375 to 0.09375
- w_up: bfloat16 [16, 1536, 4096], P('expert', 'tensor'), may hold values from -0.09375 to 0.09375
- w_down: bfloat16 [16, 1536, 4096], P('expert', 'tensor'), may hold values from -0.15625 to 0.15625
Outputs:
- d_tokens: bfloat16 [512, 4096], P(('expert', 'tensor'))
- d_probs: bfloat16 [512, 8], P(('expert', 'tensor'))
- d_gate: bfloat16 [16, 1536, 4096], P('expert', 'tensor')
- d_up: bfloat16 [16, 1536, 4096], P('expert', 'tensor')
- d_down: bfloat16 [16, 1536, 4096], P('expert', 'tensor')
The draws below stay inside these ranges and needn't reach their ends.
Inputs may be any that keep to these rules, and one draw needn't show every extreme that they name: `routes`: each token names 8 different experts. In each aligned block of 16 tokens (the tokens of one device) no expert is named by more than 12 tokens, a bound that some block reaches.
All inputs are finite; a program needn't handle non-finite values.
Results may differ from the reference program's by a relative error of at most 0.019.
Values may be sent and summed in bfloat16 or wider, within the bound.
A program may use at most 256 MiB of HBM per device.

```python
import math
import jax
import jax.numpy as jnp
import numpy as np
from jax import lax

D = 4096
FF = 1536
TOP = 8
TOK_DEV = 16
EXPERTS = 16
CAP = 12
TOKENS = 512
N_TENSOR = 4


def shard_levels(key, dims, pieces, low, high):
    level, own = 1.0, jax.random.fold_in(key, 6)
    for dim, parts in pieces:
        steps = jnp.exp(jax.random.uniform(jax.random.fold_in(own, dim), (parts,), jnp.float32, low / len(pieces), high / len(pieces)))
        level = level * jnp.repeat(steps, dims[dim] // parts).reshape([-1 if axis == dim else 1 for axis in range(len(dims))])
    return level


def deal_out(stream_key, own, number, rows, number_of, top, bound, slope):
    order = jax.random.permutation(stream_key, number_of)
    crowded, usual = shares(number_of, rows * top, bound, slope, True), shares(number_of, rows * top, bound, slope, False)
    places = jnp.arange(number_of)

    def named(lengths, offset_by):
        used = int((lengths > 0).sum())
        fixed = max(1, used // 4)
        shifted = fixed + (places - fixed + offset_by * (used - fixed)) % max(1, number_of - fixed)
        return jnp.zeros((number_of,), jnp.int32).at[order[jnp.where(places < fixed, places, shifted)]].set(jnp.asarray(lengths, jnp.int32))

    lengths = jnp.where(number % 4 == 0, named(crowded, number // 4), named(usual, number - number // 4 - 1))
    mixed = jax.random.permutation(jax.random.fold_in(own, 3), number_of)
    donor, receiver = mixed[0:number_of // 2 * 2:2], mixed[1:number_of // 2 * 2:2]
    margin = jnp.minimum(lengths[donor] - 1, bound - lengths[receiver]) // 2
    margin = jnp.where((donor == order[0]) | (receiver == order[0]) | (lengths[receiver] == 0), 0, jnp.maximum(margin, 0))
    shifted = jax.random.randint(jax.random.fold_in(own, 4), (number_of // 2,), 0, 1 << 20) % (margin + 1)
    lengths = lengths.at[donor].add(-shifted).at[receiver].add(shifted)
    items = jnp.searchsorted(jnp.cumsum(lengths), jnp.arange(rows * top), side="right").astype(jnp.int32)
    table = items.reshape(top, rows).T
    table = table[jax.random.permutation(jax.random.fold_in(own, 1), rows)]
    offset_by = jax.random.randint(jax.random.fold_in(own, 2), (rows, 1), 0, top)
    return jnp.take_along_axis(table, (jnp.arange(top)[None, :] + offset_by) % top, axis=1)


def shares(number_of, total, bound, skew, full):
    weights = [(1 << 20) // math.isqrt(rank ** skew) + 1 for rank in range(1, number_of + 1)]
    largest = bound if full else min(bound, max(-(-total // number_of), total * weights[0] // sum(weights)))
    least = 1 if total - largest >= number_of - 1 else 0
    counts, rest = [largest] + [least] * (number_of - 1), total - largest - least * (number_of - 1)
    while rest > 0:
        candidates = [i for i in range(1, number_of) if counts[i] < largest] or [i for i in range(1, number_of) if counts[i] < bound]
        mass, left = sum([weights[i] for i in candidates]), rest
        for i in candidates:
            addition = min(bound - counts[i], max(1, left * weights[i] // mass), rest)
            counts[i] = counts[i] + addition
            rest = rest - addition
    return np.array(counts)


def normal_values(stream_key, extent, scale, reach, shards=(), kind=jnp.bfloat16):
    factor_of = shard_levels(stream_key, extent, shards, -0.22, 0.18) if shards else 1.0
    values = jax.random.normal(stream_key, extent, jnp.float32) * scale * factor_of
    return jnp.minimum(jnp.maximum(values, -reach), reach).astype(kind)


def setup_inputs(seed: int = 0) -> dict:
    seeds = jax.random.split(jax.random.key(seed), 8)
    tokens = normal_values(seeds[0], (TOKENS, D), 1.0, 6.0, ((0, 32),))
    grad_out = normal_values(seeds[1], (TOKENS, D), 0.25, 1.5, ((0, 32),))
    routes_keys = jax.random.split(jax.random.fold_in(seeds[2], 1), TOKENS // TOK_DEV)
    routes_turns = jax.random.permutation(jax.random.fold_in(seeds[2], 3), TOKENS // TOK_DEV)
    routes = jax.vmap(lambda own, number: deal_out(jax.random.fold_in(seeds[2], 2), own, number, TOK_DEV, EXPERTS, TOP, CAP, 2))(routes_keys, routes_turns).reshape((TOKENS, TOP))
    gate_probs = jnp.clip(0.019897461 + 0.27893066 * jax.random.uniform(seeds[3], (TOKENS, TOP), jnp.float32) ** shard_levels(seeds[3], (TOKENS, TOP), ((0, 32),), -0.2, 0.2), 0.019897461, 0.29882812).astype(jnp.bfloat16)
    w_gate = normal_values(seeds[4], (EXPERTS, FF, D), D ** -0.5, 0.09375, ((0, 8), (1, 4)))
    w_up = normal_values(seeds[5], (EXPERTS, FF, D), D ** -0.5, 0.09375, ((0, 8), (1, 4)))
    w_down = normal_values(seeds[6], (EXPERTS, FF, D), FF ** -0.5, 0.15625, ((0, 8), (1, 4)))
    return {"tokens": tokens, "grad_out": grad_out, "routes": routes, "gate_probs": gate_probs, "w_gate": w_gate, "w_up": w_up, "w_down": w_down}


def matmul(left, right):
    return jnp.dot(left, right, preferred_element_type=jnp.float32, precision=lax.Precision.HIGHEST)


def to_bf16(values):
    return lax.optimization_barrier(values.astype(jnp.bfloat16)).astype(jnp.float32)


def reference(tokens, grad_out, routes, gate_probs, w_gate, w_up, w_down):
    blocks = TOKENS // TOK_DEV
    per_block = TOK_DEV * TOP
    route_blocks = routes.reshape(blocks, per_block).astype(jnp.int32)
    expert_ids = jnp.arange(EXPERTS, dtype=jnp.int32)
    onehot = (route_blocks[:, :, None] == expert_ids[None, None, :]).astype(jnp.int32)
    slot_rank = jnp.sum(onehot * (jnp.cumsum(onehot, axis=1) - 1), axis=2).astype(jnp.int32)
    slot_index = (route_blocks * CAP + slot_rank).astype(jnp.int32)
    row_ids = jnp.arange(TOKENS * TOP, dtype=jnp.int32).reshape(blocks, per_block)
    block_ids = jnp.broadcast_to(jnp.arange(blocks, dtype=jnp.int32)[:, None], (blocks, per_block))
    table = jnp.zeros((blocks, EXPERTS * CAP), jnp.int32).at[block_ids, slot_index].set(row_ids)
    filled = jnp.zeros((blocks, EXPERTS * CAP), jnp.float32).at[block_ids, slot_index].set(1.0)
    table = table.reshape(blocks, EXPERTS, CAP).transpose(1, 0, 2).reshape(EXPERTS, blocks * CAP)
    filled = filled.reshape(blocks, EXPERTS, CAP).transpose(1, 0, 2).reshape(EXPERTS, blocks * CAP)
    flat_probs = gate_probs.reshape(-1).astype(jnp.float32)
    block_units = FF // N_TENSOR

    def one_expert(inputs):
        row_sel, keep, weight_gate, weight_up, weight_down = inputs
        token_ids = (row_sel // TOP).astype(jnp.int32)
        x_rows = tokens[token_ids].astype(jnp.float32) * keep[:, None]
        g_rows = grad_out[token_ids].astype(jnp.float32) * keep[:, None]
        p_rows = flat_probs[row_sel] * keep
        gate_f = weight_gate.astype(jnp.float32)
        up_f = weight_up.astype(jnp.float32)
        down_f = weight_down.astype(jnp.float32)
        gate = matmul(x_rows, gate_f.T)
        up_val = matmul(x_rows, up_f.T)
        sigma = jax.nn.sigmoid(gate)
        hidden = gate * sigma * up_val
        hidden_b = to_bf16(hidden)
        back = matmul(g_rows, down_f.T)
        scaled = to_bf16(p_rows[:, None] * g_rows)
        grad_down = matmul(hidden_b.T, scaled).astype(jnp.bfloat16)
        d_hidden = p_rows[:, None] * back
        d_gate_pre = to_bf16(d_hidden * up_val * sigma * (1.0 + gate * (1.0 - sigma)))
        d_up_pre = to_bf16(d_hidden * gate * sigma)
        grad_gate = matmul(d_gate_pre.T, x_rows).astype(jnp.bfloat16)
        grad_up = matmul(d_up_pre.T, x_rows).astype(jnp.bfloat16)
        count = x_rows.shape[0]
        gate_parts = d_gate_pre.reshape(count, N_TENSOR, block_units)
        up_parts = d_up_pre.reshape(count, N_TENSOR, block_units)
        wg_parts = gate_f.reshape(N_TENSOR, block_units, D)
        wu_parts = up_f.reshape(N_TENSOR, block_units, D)
        partial_value = jnp.einsum("rtf,tfd->trd", gate_parts, wg_parts, precision=lax.Precision.HIGHEST)
        partial_value = partial_value + jnp.einsum("rtf,tfd->trd", up_parts, wu_parts, precision=lax.Precision.HIGHEST)
        row_grad = jnp.sum(to_bf16(partial_value), axis=0).astype(jnp.bfloat16)
        dprob = jnp.sum((hidden * back).reshape(count, N_TENSOR, block_units), axis=2)
        row_dprob = jnp.sum(to_bf16(dprob), axis=1).astype(jnp.bfloat16)
        return row_grad, row_dprob, grad_gate, grad_up, grad_down

    row_grad, row_dprob, d_gate, d_up, d_down = lax.map(one_expert, (table, filled, w_gate, w_up, w_down))
    flat_rows = table.reshape(-1)
    flat_keep = filled.reshape(-1)
    token_of = (flat_rows // TOP).astype(jnp.int32)
    grads = row_grad.reshape(-1, D).astype(jnp.float32) * flat_keep[:, None]
    d_tokens = jnp.zeros((TOKENS, D), jnp.float32).at[token_of].add(grads).astype(jnp.bfloat16)
    dprobs = row_dprob.reshape(-1).astype(jnp.float32) * flat_keep
    d_probs = jnp.zeros((TOKENS * TOP,), jnp.float32).at[flat_rows].add(dprobs)
    d_probs = d_probs.reshape(TOKENS, TOP).astype(jnp.bfloat16)
    return (d_tokens, d_probs, d_gate, d_up, d_down)
```

```python
import jax
import jax.numpy as jnp
from jax import lax
from jax.sharding import PartitionSpec as P

AXES = ("expert", "tensor")


def per_device(tokens, grad_out, routes, gate_probs, w_gate, w_up, w_down):
    local, units, width = w_gate.shape
    first = lax.axis_index("expert") * local
    mine = first + jnp.arange(local, dtype=jnp.int32)
    owners = lax.axis_size("expert")
    ids = jnp.arange(local * owners, dtype=jnp.int32)
    hit = routes[:, :, None] == ids[None, None, :]
    table = jnp.sum(jnp.where(hit, gate_probs[:, :, None].astype(jnp.float32), 0.0), axis=1)
    table = table.astype(jnp.bfloat16)
    rows_x = lax.all_gather(tokens, AXES, axis=0, tiled=True)
    rows_g = lax.all_gather(grad_out, AXES, axis=0, tiled=True)
    probs = lax.all_gather(table, AXES, axis=0, tiled=True)
    probs = lax.dynamic_slice_in_dim(probs, first, local, axis=1).astype(jnp.float32)
    count = rows_x.shape[0]
    wg = w_gate.reshape(local * units, width)
    wu = w_up.reshape(local * units, width)
    wd = w_down.reshape(local * units, width)
    nt = (((1,), (1,)), ((), ()))
    tn = (((0,), (0,)), ((), ()))
    f32 = jnp.float32
    gate = lax.dot_general(rows_x, wg, nt, preferred_element_type=f32)
    up = lax.dot_general(rows_x, wu, nt, preferred_element_type=f32)
    back = lax.dot_general(rows_g, wd, nt, preferred_element_type=f32)
    sigma = jax.nn.sigmoid(gate)
    act = gate * sigma
    hidden = act * up
    p = jnp.broadcast_to(probs[:, :, None], (count, local, units)).reshape(count, local * units)
    d_hidden = p * back
    dgp = (d_hidden * up * sigma * (1.0 + gate * (1.0 - sigma))).astype(jnp.bfloat16)
    dup = (d_hidden * act).astype(jnp.bfloat16)
    hs = (hidden * p).astype(jnp.bfloat16)
    dprob = jnp.sum((hidden * back).reshape(count, local, units), axis=2)
    part = lax.dot_general(dgp, wg, (((1,), (0,)), ((), ())), preferred_element_type=f32)
    part = part + lax.dot_general(dup, wu, (((1,), (0,)), ((), ())), preferred_element_type=f32)
    d_tokens = lax.psum_scatter(part.astype(jnp.bfloat16), AXES, scatter_dimension=0, tiled=True)
    d_gate = lax.dot_general(dgp, rows_x, tn, preferred_element_type=f32).astype(jnp.bfloat16)
    d_up = lax.dot_general(dup, rows_x, tn, preferred_element_type=f32).astype(jnp.bfloat16)
    d_down = lax.dot_general(hs, rows_g, tn, preferred_element_type=f32).astype(jnp.bfloat16)
    wide = lax.dynamic_update_slice(jnp.zeros((count, local * owners), f32), dprob, (0, first))
    mineprob = lax.psum_scatter(wide.astype(jnp.bfloat16), AXES, scatter_dimension=0, tiled=True)
    d_probs = jnp.sum(jnp.where(hit, mineprob.astype(f32)[:, None, :], 0.0), axis=2).astype(jnp.bfloat16)
    shape = (local, units, width)
    return (d_tokens, d_probs, d_gate.reshape(shape), d_up.reshape(shape), d_down.reshape(shape))


def solution(mesh):
    tok = P(AXES, None)
    wt = P("expert", "tensor", None)
    return jax.shard_map(
        per_device, mesh=mesh, in_specs=(tok, tok, tok, tok, wt, wt, wt),
        out_specs=(tok, tok, wt, wt, wt), check_vma=False
    )
```

```python
import jax
import jax.numpy as jnp
from jax import lax
from jax.experimental import pallas as pl
from jax.experimental.pallas import tpu as pltpu
from jax.sharding import PartitionSpec as P

AXES = ("expert", "tensor")
CHUNK = 512
LAG = 2
NT = (((1,), (1,)), ((), ()))
F32 = jnp.float32
B16 = jnp.bfloat16


def gather_and_send_back(tensor, tok, width, local, units):
    chunks = width // CHUNK
    half = CHUNK // 2
    group = tensor * tok
    hid = local * units
    others = tensor - 1

    def body(x_in, g_in, t_in, wg_in, wu_in, wd_in,
             dx_out, dp_out, xs_out, gs_out, dg_out, du_out, hs_out,
             xbuf, gbuf, tbuf, wgb, wub, wdb, gate, up, back, dgp, dup, hs,
             pbuf, sbuf, ybuf, xb, azb, cxb, czb, cyb,
             dpb, dps, dpy, dpx, dpz,
             lsem, wsem, osem, hsem,
             ax_s, ax_r, ag_s, ag_r, ss_s, ss_r, sa_s, sa_r, sc_s, sc_r):
        e = lax.axis_index("expert")
        z = lax.axis_index("tensor")
        core = e % 2
        bx = (e // 2) % 2
        by = e // 4
        to_s, to_x, to_y = 1 - 2 * core, 2 - 4 * bx, 4 - 8 * by
        e_s, e_x, e_y, e_d = e + to_s, e + to_x, e + to_y, e + to_x + to_y
        mine = (e, e_x, e_y, e_d)

        def dev(expert, place):
            return {"expert": expert, "tensor": place}

        sib, xpeer, ypeer = dev(e_s, z), dev(e_x, z), dev(e_y, z)
        zpeer = [None] + [dev(e, (z + k) % tensor) for k in range(1, tensor)]
        zfrom = [None] + [(z + tensor - k) % tensor for k in range(1, tensor)]
        zto = [None] + [(z + k) % tensor for k in range(1, tensor)]

        def grp(expert):
            return pl.ds(pl.multiple_of(expert * group, group), group)

        def row(expert, place):
            return pl.ds(pl.multiple_of((expert * tensor + place) * tok, tok), tok)

        def rc(src, dst, s, r, to):
            return pltpu.make_async_remote_copy(
                src_ref=src, dst_ref=dst, send_sem=s, recv_sem=r, device_id=to,
                device_id_type=pl.DeviceIdType.MESH)

        own = row(e, z)
        for c in range(chunks):
            cols = pl.ds(c * CHUNK, CHUNK)
            pltpu.make_async_copy(x_in.at[:, cols], xbuf.at[c, own], lsem.at[0, c]).start()
            pltpu.make_async_copy(g_in.at[:, cols], gbuf.at[c, own], lsem.at[1, c]).start()
        pltpu.make_async_copy(t_in, tbuf.at[0, own], lsem.at[0, chunks]).start()

        barrier = pltpu.get_barrier_semaphore()
        for to in [sib, xpeer, ypeer] + zpeer[1:]:
            pl.semaphore_signal(barrier, inc=1, device_id=to, device_id_type=pl.DeviceIdType.MESH)
        for c in range(chunks):
            cols = pl.ds(c * CHUNK, CHUNK)
            for n, (src, dst) in enumerate(((wg_in, wgb), (wu_in, wub), (wd_in, wdb))):
                pltpu.make_async_copy(src.at[:, cols], dst.at[c], wsem.at[n, c]).start()
        gate[...] = jnp.zeros_like(gate)
        up[...] = jnp.zeros_like(up)
        back[...] = jnp.zeros_like(back)
        for c in range(chunks):
            cols = pl.ds(c * CHUNK, CHUNK)
            pltpu.make_async_copy(x_in.at[:, cols], xbuf.at[c, own], lsem.at[0, c]).wait()
            pltpu.make_async_copy(g_in.at[:, cols], gbuf.at[c, own], lsem.at[1, c]).wait()
        pltpu.make_async_copy(t_in, tbuf.at[0, own], lsem.at[0, chunks]).wait()
        pl.semaphore_wait(barrier, 3 + others)

        def a_z(buf, i, q, k, source=False):
            rows = row(e, zfrom[k]) if source else own
            return rc(buf.at[i, rows], buf.at[i, rows], ax_s.at[q, k - 1], ax_r.at[q, k - 1], zpeer[k])

        def a_g(buf, i, q, n, expert, to):
            rows = grp(expert)
            return rc(buf.at[i, rows], buf.at[i, rows], ax_s.at[q, others + n], ax_r.at[q, others + n], to)

        a_sends = ((0, e, xpeer), (1, e, ypeer), (2, e_x, ypeer), (3, e, sib), (4, e_x, sib), (5, e_y, sib), (6, e_d, sib))
        a_recvs = ((0, e_x, xpeer), (1, e_y, ypeer), (2, e_d, ypeer),
                   (3, e_s, sib), (4, e_s + to_x, sib), (5, e_s + to_y, sib), (6, e_s + to_x + to_y, sib))

        def a_send(buf, i, q, n):
            a_g(buf, i, q, *a_sends[n]).start()

        def a_recv(buf, i, q, n):
            a_g(buf, i, q, *a_recvs[n]).wait_recv()

        def gather_a(s, buf, i, q):
            if s == 0:
                for k in range(1, tensor):
                    a_z(buf, i, q, k).start()
            if s == 1:
                for k in range(1, tensor):
                    a_z(buf, i, q, k, True).wait_recv()
                for n in (0, 1, 3):
                    a_send(buf, i, q, n)
            if s == 2:
                a_recv(buf, i, q, 0)
                for n in (2, 4):
                    a_send(buf, i, q, n)
            if s == 3:
                a_recv(buf, i, q, 1)
                a_send(buf, i, q, 5)
                a_recv(buf, i, q, 2)
                a_send(buf, i, q, 6)
            if s == 4:
                for n in (3, 4, 5, 6):
                    a_recv(buf, i, q, n)

        def gather_a_drain(buf, i, q):
            for k in range(1, tensor):
                a_z(buf, i, q, k).wait_send()
            for n in range(7):
                a_g(buf, i, q, *a_sends[n]).wait_send()

        def c_y(i, source=False):
            rows = row(e_y, z) if source else own
            return rc(gbuf.at[i, rows], gbuf.at[i, rows], ag_s.at[i, 0], ag_r.at[i, 0], ypeer)

        def c_z(i, k, n, source=False):
            rows = row((e, e_y)[n], zfrom[k] if source else z)
            at = 1 + n * others + k - 1
            return rc(gbuf.at[i, rows], gbuf.at[i, rows], ag_s.at[i, at], ag_r.at[i, at], zpeer[k])

        c_base = 1 + 2 * others

        def c_g(i, n, expert, to):
            rows = grp(expert)
            return rc(gbuf.at[i, rows], gbuf.at[i, rows], ag_s.at[i, c_base + n], ag_r.at[i, c_base + n], to)

        c_sends = ((0, e, xpeer), (1, e_y, xpeer), (2, e, sib), (3, e_y, sib), (4, e_x, sib), (5, e_d, sib))
        c_recvs = ((0, e_x, xpeer), (1, e_d, xpeer), (2, e_s, sib), (3, e_s + to_y, sib),
                   (4, e_s + to_x, sib), (5, e_s + to_x + to_y, sib))

        def gather_c(s, i):
            if s == 0:
                c_y(i).start()
                for k in range(1, tensor):
                    c_z(i, k, 0).start()
            if s == 1:
                c_y(i, True).wait_recv()
                for k in range(1, tensor):
                    c_z(i, k, 1).start()
            if s == 2:
                for k in range(1, tensor):
                    c_z(i, k, 0, True).wait_recv()
                for n in (0, 2):
                    c_g(i, *c_sends[n]).start()
                for k in range(1, tensor):
                    c_z(i, k, 1, True).wait_recv()
                for n in (1, 3):
                    c_g(i, *c_sends[n]).start()
            if s == 3:
                for n in (0, 1):
                    c_g(i, *c_recvs[n]).wait_recv()
                    c_g(i, *c_sends[n + 4]).start()
            if s == 4:
                for n in (2, 3, 4, 5):
                    c_g(i, *c_recvs[n]).wait_recv()

        def gather_c_drain(i):
            c_y(i).wait_send()
            for k in range(1, tensor):
                c_z(i, k, 0).wait_send()
                c_z(i, k, 1).wait_send()
            for n in range(6):
                c_g(i, *c_sends[n]).wait_send()

        def save_x(j):
            at = pl.ds(pl.multiple_of(j * CHUNK, CHUNK), CHUNK)
            return (pltpu.make_async_copy(xbuf.at[j], xs_out.at[:, at], osem.at[0, j]),
                    pltpu.make_async_copy(gbuf.at[j], gs_out.at[:, at], osem.at[1, j]))

        steps = chunks + 4 * LAG

        def gather_step(t, carry):
            for s in range(5):
                j = t - s * LAG

                @pl.when(t == s * LAG)
                def _():
                    gather_a(s, tbuf, 0, chunks)

                @pl.when(jnp.logical_and(j >= 0, j < chunks))
                def _():
                    gather_a(s, xbuf, j, j)
                    gather_c(s, j)
                    if s == 4:
                        for c in save_x(j):
                            c.start()
                        for n, (src, dst) in enumerate(((wg_in, wgb), (wu_in, wub), (wd_in, wdb))):
                            pltpu.make_async_copy(src.at[:, pl.ds(0, CHUNK)], dst.at[j], wsem.at[n, j]).wait()
                        gate[...] += lax.dot_general(xbuf[j], wgb[j], NT, preferred_element_type=F32)
                        up[...] += lax.dot_general(xbuf[j], wub[j], NT, preferred_element_type=F32)
                        back[...] += lax.dot_general(gbuf[j], wdb[j], NT, preferred_element_type=F32)
            return carry

        lax.fori_loop(0, steps, gather_step, 0)

        block = 32
        lane = lax.broadcasted_iota(jnp.int32, (block, tbuf.shape[2]), 1)

        def hidden_step(b, carry):
            rows = pl.ds(pl.multiple_of(b * block, block), block)
            table = tbuf[0, rows, :].astype(F32)
            placed = jnp.zeros((block, tbuf.shape[2]), F32)
            for n in range(local):
                cols = pl.ds(n * units, units)
                here = lane == e * local + n
                p = jnp.sum(jnp.where(here, table, 0.0), axis=1, keepdims=True)
                gv, uv, bv = gate[rows, cols], up[rows, cols], back[rows, cols]
                sg = jax.nn.sigmoid(gv)
                act = gv * sg
                hv = act * uv
                pb = p * bv
                dgp[rows, cols] = (pb * uv * sg * (1.0 + gv * (1.0 - sg))).astype(B16)
                dup[rows, cols] = (pb * act).astype(B16)
                hs[rows, cols] = (hv * p).astype(B16)
                placed = placed + jnp.where(here, jnp.sum(hv * bv, axis=1, keepdims=True), 0.0)
            dpb[0, rows, :] = placed.astype(B16)
            return carry

        lax.fori_loop(0, gate.shape[0] // block, hidden_step, 0)
        saves = [pltpu.make_async_copy(a, b, hsem.at[n])
                 for n, (a, b) in enumerate(((dgp, dg_out), (dup, du_out), (hs, hs_out)))]
        for c in saves:
            c.start()

        order = (3, 2, 1, 0)

        def slot(n):
            return pl.ds(n * group, group)

        def back_s(p, d, i, q, n):
            return rc(p.at[i, grp(mine[n] + to_s)], d.at[i, slot(n)], ss_s.at[q, n], ss_r.at[q, n], sib)

        def merge_s(p, d, i, q):
            for n in order:
                back_s(p, d, i, q, n).wait_recv()
                p[i, grp(mine[n]), :] = (p[i, grp(mine[n]), :].astype(F32)
                                         + d[i, slot(n), :].astype(F32)).astype(B16)

        def add(p, i, rows, cols, term):
            p[i, rows, cols] = (p[i, rows, cols].astype(F32) + term).astype(B16)

        def a_back(p, y_, x_, z_, i, q, cols, kind, n):
            if kind == 0:
                return rc(p.at[i, grp((e_y, e_d)[n]), cols], y_.at[i, slot(n)], sa_s.at[q, n], sa_r.at[q, n], ypeer)
            if kind == 1:
                return rc(p.at[i, grp(e_x), cols], x_.at[i], sa_s.at[q, 2], sa_r.at[q, 2], xpeer)
            return rc(p.at[i, row(e, zto[n]), cols], z_.at[i, pl.ds((n - 1) * tok, tok)],
                      sa_s.at[q, 2 + n], sa_r.at[q, 2 + n], zpeer[n])

        def scatter_a(s, bufs, i, q, cols, out, at):
            p, y_, x_, z_ = bufs
            args = (p, y_, x_, z_, i, q, cols)
            if s == 1:
                for n in (1, 0):
                    a_back(*args, 0, n).start()
            if s == 2:
                for n in (1, 0):
                    a_back(*args, 0, n).wait_recv()
                    add(p, i, grp((e, e_x)[n]), cols, y_[i, slot(n), :].astype(F32))
                    if n == 1:
                        a_back(*args, 1, 0).start()
            if s == 3:
                a_back(*args, 1, 0).wait_recv()
                add(p, i, grp(e), cols, x_[i].astype(F32))
                for k in range(1, tensor):
                    a_back(*args, 2, k).start()
            if s == 4:
                total = p[i, own, cols].astype(F32)
                for k in range(1, tensor):
                    a_back(*args, 2, k).wait_recv()
                    total = total + z_[i, pl.ds((k - 1) * tok, tok), :].astype(F32)
                out[:, at] = total.astype(B16)

        def scatter_a_drain(bufs, i, q, cols):
            args = (*bufs, i, q, cols)
            for n in (0, 1):
                a_back(*args, 0, n).wait_send()
            a_back(*args, 1, 0).wait_send()
            for k in range(1, tensor):
                a_back(*args, 2, k).wait_send()

        ccols = pl.ds(half, half)

        def c_back(i, kind, n, m=0):
            if kind == 0:
                return rc(pbuf.at[i, grp((e_x, e_d)[n]), ccols], cxb.at[i, slot(n)], sc_s.at[i, n], sc_r.at[i, n], xpeer)
            if kind == 1:
                at = m * others + n - 1
                return rc(pbuf.at[i, row((e, e_y)[m], zto[n]), ccols], czb.at[i, pl.ds(at * tok, tok)],
                          sc_s.at[i, 2 + at], sc_r.at[i, 2 + at], zpeer[n])
            at = 2 + 2 * others
            return rc(pbuf.at[i, row(e_y, z), ccols], cyb.at[i], sc_s.at[i, at], sc_r.at[i, at], ypeer)

        def scatter_c(s, i, out, at):
            if s == 1:
                for n in (1, 0):
                    c_back(i, 0, n).start()
            if s == 2:
                for n in (1, 0):
                    c_back(i, 0, n).wait_recv()
                    add(pbuf, i, grp((e, e_y)[n]), ccols, cxb[i, slot(n), :].astype(F32))
                    for k in range(1, tensor):
                        c_back(i, 1, k, n).start()
            if s == 3:
                for m in (1, 0):
                    total = jnp.zeros((tok, half), F32)
                    for k in range(1, tensor):
                        c_back(i, 1, k, m).wait_recv()
                        total = total + czb[i, pl.ds((m * others + k - 1) * tok, tok), :].astype(F32)
                    add(pbuf, i, row((e, e_y)[m], z), ccols, total)
                    if m == 1:
                        c_back(i, 2, 0).start()
            if s == 4:
                c_back(i, 2, 0).wait_recv()
                out[:, at] = (pbuf[i, own, ccols].astype(F32) + cyb[i].astype(F32)).astype(B16)

        def scatter_c_drain(i):
            for n in (0, 1):
                c_back(i, 0, n).wait_send()
            for m in (0, 1):
                for k in range(1, tensor):
                    c_back(i, 1, k, m).wait_send()
            c_back(i, 2, 0).wait_send()

        acols = pl.ds(0, half)
        big = (pbuf, ybuf, xb, azb)
        small = (dpb, dpy, dpx, dpz)
        all_cols = pl.ds(0, tbuf.shape[2])

        def scatter_step(t, carry):
            @pl.when(t < chunks)
            def _():
                part = jnp.dot(dgp[...], wgb[t], preferred_element_type=F32)
                part = part + jnp.dot(dup[...], wub[t], preferred_element_type=F32)
                pbuf[t] = part.astype(B16)

            for s in range(5):
                j = t - s * LAG

                @pl.when(t == s * LAG)
                def _():
                    if s == 0:
                        for n in order:
                            back_s(dpb, dps, 0, chunks, n).start()
                    if s == 1:
                        merge_s(dpb, dps, 0, chunks)
                    scatter_a(s, small, 0, chunks, all_cols, dp_out, all_cols)

                @pl.when(jnp.logical_and(j >= 0, j < chunks))
                def _():
                    if s == 0:
                        for n in order:
                            back_s(pbuf, sbuf, j, j, n).start()
                    if s == 1:
                        merge_s(pbuf, sbuf, j, j)
                    a_at = pl.ds(pl.multiple_of(j * CHUNK, CHUNK), half)
                    c_at = pl.ds(pl.multiple_of(j * CHUNK + half, half), half)
                    scatter_a(s, big, j, j, acols, dx_out, a_at)
                    scatter_c(s, j, dx_out, c_at)
            return carry

        lax.fori_loop(0, steps, scatter_step, 0)

        gather_a_drain(tbuf, 0, chunks)
        for n in order:
            back_s(dpb, dps, 0, chunks, n).wait_send()
        scatter_a_drain(small, 0, chunks, all_cols)

        def drain(j, carry):
            gather_a_drain(xbuf, j, j)
            gather_c_drain(j)
            for n in order:
                back_s(pbuf, sbuf, j, j, n).wait_send()
            scatter_a_drain(big, j, j, acols)
            scatter_c_drain(j)
            for c in save_x(j):
                c.wait()
            return carry

        lax.fori_loop(0, chunks, drain, 0)
        for c in saves:
            c.wait()

    return body


def fused(tokens, grad_out, table, wg, wu, wd, tensor, local, units):
    tok, width = tokens.shape
    lanes = table.shape[1]
    owners = lax.axis_size("expert")
    rows = owners * tensor * tok
    hid = local * units
    chunks = width // CHUNK
    half = CHUNK // 2
    mid = owners // 2 * tensor * tok
    two, one = 2 * tensor * tok, tensor * tok
    oth = tensor - 1
    V = pltpu.VMEM
    dma = pltpu.SemaphoreType.DMA
    scratch = [
        V((chunks, rows, CHUNK), B16), V((chunks, rows, CHUNK), B16), V((1, rows, lanes), B16),
        V((chunks, hid, CHUNK), B16), V((chunks, hid, CHUNK), B16), V((chunks, hid, CHUNK), B16),
        V((rows, hid), F32), V((rows, hid), F32), V((rows, hid), F32),
        V((rows, hid), B16), V((rows, hid), B16), V((rows, hid), B16),
        V((chunks, rows, CHUNK), B16), V((chunks, mid, CHUNK), B16),
        V((chunks, two, half), B16), V((chunks, one, half), B16), V((chunks, oth * tok, half), B16),
        V((chunks, two, half), B16), V((chunks, 2 * oth * tok, half), B16), V((chunks, tok, half), B16),
        V((1, rows, lanes), B16), V((1, mid, lanes), B16), V((1, two, lanes), B16), V((1, one, lanes), B16),
        V((1, oth * tok, lanes), B16),
        dma((2, chunks + 1)), dma((3, chunks)), dma((2, chunks)), dma((3,)),
        dma((chunks + 1, oth + 7)), dma((chunks + 1, oth + 7)),
        dma((chunks, 2 * oth + 7)), dma((chunks, 2 * oth + 7)),
        dma((chunks + 1, 4)), dma((chunks + 1, 4)),
        dma((chunks + 1, 3 + oth)), dma((chunks + 1, 3 + oth)),
        dma((chunks, 3 + 2 * oth)), dma((chunks, 3 + 2 * oth)),
    ]
    any_, vm = pl.BlockSpec(memory_space=pl.ANY), pl.BlockSpec(memory_space=pltpu.VMEM)
    sd = jax.ShapeDtypeStruct
    return pl.pallas_call(
        gather_and_send_back(tensor, tok, width, local, units),
        out_shape=(sd((tok, width), B16), sd((tok, lanes), B16), sd((rows, width), B16), sd((rows, width), B16),
                   sd((rows, hid), B16), sd((rows, hid), B16), sd((rows, hid), B16)),
        in_specs=[any_] * 6,
        out_specs=(vm, vm) + (any_,) * 5,
        scratch_shapes=scratch,
        compiler_params=pltpu.CompilerParams(collective_id=0, has_side_effects=True, vmem_limit_bytes=60 * 1024 * 1024),
        cost_estimate=pl.CostEstimate(flops=10 * rows * hid * width, transcendentals=rows * hid,
                                      bytes_accessed=6 * hid * width + 8 * rows * width),
        name="gather_and_send_back",
    )(tokens, grad_out, table, wg, wu, wd)


def with_kernel(tokens, grad_out, routes, gate_probs, w_gate, w_up, w_down):
    local, units, width = w_gate.shape
    tensor = lax.axis_size("tensor")
    ids = jnp.arange(128, dtype=jnp.int32)
    hit = routes[:, :, None] == ids[None, None, :]
    table = jnp.sum(jnp.where(hit, gate_probs[:, :, None].astype(F32), 0.0), axis=1).astype(B16)
    flat = [w.reshape(local * units, width) for w in (w_gate, w_up, w_down)]
    d_tokens, dp, xs, gs, dgp, dup, hs = fused(tokens, grad_out, table, *flat, tensor, local, units)
    tn = (((0,), (0,)), ((), ()))
    shape = (local, units, width)
    d_gate = lax.dot_general(dgp, xs, tn, preferred_element_type=F32).astype(B16).reshape(shape)
    d_up = lax.dot_general(dup, xs, tn, preferred_element_type=F32).astype(B16).reshape(shape)
    d_down = lax.dot_general(hs, gs, tn, preferred_element_type=F32).astype(B16).reshape(shape)
    d_probs = jnp.sum(jnp.where(hit, dp.astype(F32)[:, None, :], 0.0), axis=2).astype(B16)
    return (d_tokens, d_probs, d_gate, d_up, d_down)


def per_device(tokens, grad_out, routes, gate_probs, w_gate, w_up, w_down):
    local, units, width = w_gate.shape
    first = lax.axis_index("expert") * local
    mine = first + jnp.arange(local, dtype=jnp.int32)
    owners = lax.axis_size("expert")
    ids = jnp.arange(local * owners, dtype=jnp.int32)
    hit = routes[:, :, None] == ids[None, None, :]
    table = jnp.sum(jnp.where(hit, gate_probs[:, :, None].astype(jnp.float32), 0.0), axis=1)
    table = table.astype(jnp.bfloat16)
    rows_x = lax.all_gather(tokens, AXES, axis=0, tiled=True)
    rows_g = lax.all_gather(grad_out, AXES, axis=0, tiled=True)
    probs = lax.all_gather(table, AXES, axis=0, tiled=True)
    probs = lax.dynamic_slice_in_dim(probs, first, local, axis=1).astype(jnp.float32)
    count = rows_x.shape[0]
    wg = w_gate.reshape(local * units, width)
    wu = w_up.reshape(local * units, width)
    wd = w_down.reshape(local * units, width)
    nt = (((1,), (1,)), ((), ()))
    tn = (((0,), (0,)), ((), ()))
    f32 = jnp.float32
    gate = lax.dot_general(rows_x, wg, nt, preferred_element_type=f32)
    up = lax.dot_general(rows_x, wu, nt, preferred_element_type=f32)
    back = lax.dot_general(rows_g, wd, nt, preferred_element_type=f32)
    sigma = jax.nn.sigmoid(gate)
    act = gate * sigma
    hidden = act * up
    p = jnp.broadcast_to(probs[:, :, None], (count, local, units)).reshape(count, local * units)
    d_hidden = p * back
    dgp = (d_hidden * up * sigma * (1.0 + gate * (1.0 - sigma))).astype(jnp.bfloat16)
    dup = (d_hidden * act).astype(jnp.bfloat16)
    hs = (hidden * p).astype(jnp.bfloat16)
    dprob = jnp.sum((hidden * back).reshape(count, local, units), axis=2)
    part = lax.dot_general(dgp, wg, (((1,), (0,)), ((), ())), preferred_element_type=f32)
    part = part + lax.dot_general(dup, wu, (((1,), (0,)), ((), ())), preferred_element_type=f32)
    d_tokens = lax.psum_scatter(part.astype(jnp.bfloat16), AXES, scatter_dimension=0, tiled=True)
    d_gate = lax.dot_general(dgp, rows_x, tn, preferred_element_type=f32).astype(jnp.bfloat16)
    d_up = lax.dot_general(dup, rows_x, tn, preferred_element_type=f32).astype(jnp.bfloat16)
    d_down = lax.dot_general(hs, rows_g, tn, preferred_element_type=f32).astype(jnp.bfloat16)
    wide = lax.dynamic_update_slice(jnp.zeros((count, local * owners), f32), dprob, (0, first))
    mineprob = lax.psum_scatter(wide.astype(jnp.bfloat16), AXES, scatter_dimension=0, tiled=True)
    d_probs = jnp.sum(jnp.where(hit, mineprob.astype(f32)[:, None, :], 0.0), axis=2).astype(jnp.bfloat16)
    shape = (local, units, width)
    return (d_tokens, d_probs, d_gate.reshape(shape), d_up.reshape(shape), d_down.reshape(shape))


def solution(mesh):
    tok = P(AXES, None)
    wt = P("expert", "tensor", None)

    def program(tokens, grad_out, routes, gate_probs, w_gate, w_up, w_down):
        small = tokens.shape[0] <= 512 and mesh.shape["expert"] == 8 and mesh.shape["tensor"] > 1
        small = small and tokens.shape[0] // mesh.size == 16 and tokens.shape[1] % CHUNK == 0
        small = small and w_gate.shape[0] <= 128 and w_gate.shape[0] == 16
        small = small and w_gate.shape[1] // mesh.shape["tensor"] <= 384 and w_gate.shape[2] <= 4096
        return jax.shard_map(
            with_kernel if small else per_device, mesh=mesh, in_specs=(tok, tok, tok, tok, wt, wt, wt),
            out_specs=(tok, tok, wt, wt, wt), check_vma=False
        )(tokens, grad_out, routes, gate_probs, w_gate, w_up, w_down)

    return program
```

```python
import jax
import jax.numpy as jnp
from jax import lax
from jax.experimental import pallas as pl
from jax.experimental.pallas import tpu as pltpu
from jax.sharding import PartitionSpec as P

AXES = ("expert", "tensor")
CHUNK = 512
LAG = 2
NT = (((1,), (1,)), ((), ()))
F32 = jnp.float32
B16 = jnp.bfloat16


def gather_and_send_back(tensor, tok, width, local, units):
    chunks = width // CHUNK
    half = CHUNK // 2
    group = tensor * tok
    hid = local * units
    others = tensor - 1

    def body(x_in, g_in, t_in, wg_in, wu_in, wd_in,
             dx_out, dp_out, xs_out, gs_out, dg_out, du_out, hs_out,
             xbuf, gbuf, tbuf, wgb, wub, wdb, gate, up, back, dgp, dup, hs,
             pbuf, sbuf, ybuf, xb, azb, cxb, czb, cyb,
             dpb, dps, dpy, dpx, dpz,
             lsem, wsem, osem, hsem,
             ax_s, ax_r, ag_s, ag_r, ss_s, ss_r, sa_s, sa_r, sc_s, sc_r):
        e = lax.axis_index("expert")
        z = lax.axis_index("tensor")
        core = e % 2
        bx = (e // 2) % 2
        by = e // 4
        to_s, to_x, to_y = 1 - 2 * core, 2 - 4 * bx, 4 - 8 * by
        e_s, e_x, e_y, e_d = e + to_s, e + to_x, e + to_y, e + to_x + to_y
        mine = (e, e_x, e_y, e_d)

        def dev(expert, place):
            return {"expert": expert, "tensor": place}

        sib, xpeer, ypeer = dev(e_s, z), dev(e_x, z), dev(e_y, z)
        zpeer = [None] + [dev(e, (z + k) % tensor) for k in range(1, tensor)]
        zfrom = [None] + [(z + tensor - k) % tensor for k in range(1, tensor)]
        zto = [None] + [(z + k) % tensor for k in range(1, tensor)]

        def grp(expert):
            return pl.ds(pl.multiple_of(expert * group, group), group)

        def row(expert, place):
            return pl.ds(pl.multiple_of((expert * tensor + place) * tok, tok), tok)

        def rc(src, dst, s, r, to):
            return pltpu.make_async_remote_copy(
                src_ref=src, dst_ref=dst, send_sem=s, recv_sem=r, device_id=to,
                device_id_type=pl.DeviceIdType.MESH)

        own = row(e, z)
        for c in range(chunks):
            cols = pl.ds(c * CHUNK, CHUNK)
            pltpu.make_async_copy(x_in.at[:, cols], xbuf.at[c, own], lsem.at[0, c]).start()
            pltpu.make_async_copy(g_in.at[:, cols], gbuf.at[c, own], lsem.at[1, c]).start()
        pltpu.make_async_copy(t_in, tbuf.at[0, own], lsem.at[0, chunks]).start()

        barrier = pltpu.get_barrier_semaphore()
        for to in [sib, xpeer, ypeer] + zpeer[1:]:
            pl.semaphore_signal(barrier, inc=1, device_id=to, device_id_type=pl.DeviceIdType.MESH)
        for c in range(chunks):
            cols = pl.ds(c * CHUNK, CHUNK)
            for n, (src, dst) in enumerate(((wg_in, wgb), (wu_in, wub), (wd_in, wdb))):
                pltpu.make_async_copy(src.at[:, cols], dst.at[c], wsem.at[n, c]).start()
        gate[...] = jnp.zeros_like(gate)
        up[...] = jnp.zeros_like(up)
        back[...] = jnp.zeros_like(back)
        for c in range(chunks):
            cols = pl.ds(c * CHUNK, CHUNK)
            pltpu.make_async_copy(x_in.at[:, cols], xbuf.at[c, own], lsem.at[0, c]).wait()
            pltpu.make_async_copy(g_in.at[:, cols], gbuf.at[c, own], lsem.at[1, c]).wait()
        pltpu.make_async_copy(t_in, tbuf.at[0, own], lsem.at[0, chunks]).wait()
        pl.semaphore_wait(barrier, 3 + others)

        def a_z(buf, i, q, k, source=False):
            rows = row(e, zfrom[k]) if source else own
            return rc(buf.at[i, rows], buf.at[i, rows], ax_s.at[q, k - 1], ax_r.at[q, k - 1], zpeer[k])

        def a_g(buf, i, q, n, expert, to):
            rows = grp(expert)
            return rc(buf.at[i, rows], buf.at[i, rows], ax_s.at[q, others + n], ax_r.at[q, others + n], to)

        a_sends = ((0, e, xpeer), (1, e, ypeer), (2, e_x, ypeer), (3, e, sib), (4, e_x, sib), (5, e_y, sib), (6, e_d, sib))
        a_recvs = ((0, e_x, xpeer), (1, e_y, ypeer), (2, e_d, ypeer),
                   (3, e_s, sib), (4, e_s + to_x, sib), (5, e_s + to_y, sib), (6, e_s + to_x + to_y, sib))

        def a_send(buf, i, q, n):
            a_g(buf, i, q, *a_sends[n]).start()

        def a_recv(buf, i, q, n):
            a_g(buf, i, q, *a_recvs[n]).wait_recv()

        def gather_a(s, buf, i, q):
            if s == 0:
                for k in range(1, tensor):
                    a_z(buf, i, q, k).start()
            if s == 1:
                for k in range(1, tensor):
                    a_z(buf, i, q, k, True).wait_recv()
                for n in (0, 1, 3):
                    a_send(buf, i, q, n)
            if s == 2:
                a_recv(buf, i, q, 0)
                for n in (2, 4):
                    a_send(buf, i, q, n)
            if s == 3:
                a_recv(buf, i, q, 1)
                a_send(buf, i, q, 5)
                a_recv(buf, i, q, 2)
                a_send(buf, i, q, 6)
            if s == 4:
                for n in (3, 4, 5, 6):
                    a_recv(buf, i, q, n)

        def gather_a_drain(buf, i, q):
            for k in range(1, tensor):
                a_z(buf, i, q, k).wait_send()
            for n in range(7):
                a_g(buf, i, q, *a_sends[n]).wait_send()

        def c_y(i, source=False):
            rows = row(e_y, z) if source else own
            return rc(gbuf.at[i, rows], gbuf.at[i, rows], ag_s.at[i, 0], ag_r.at[i, 0], ypeer)

        def c_z(i, k, n, source=False):
            rows = row((e, e_y)[n], zfrom[k] if source else z)
            at = 1 + n * others + k - 1
            return rc(gbuf.at[i, rows], gbuf.at[i, rows], ag_s.at[i, at], ag_r.at[i, at], zpeer[k])

        c_base = 1 + 2 * others

        def c_g(i, n, expert, to):
            rows = grp(expert)
            return rc(gbuf.at[i, rows], gbuf.at[i, rows], ag_s.at[i, c_base + n], ag_r.at[i, c_base + n], to)

        c_sends = ((0, e, xpeer), (1, e_y, xpeer), (2, e, sib), (3, e_y, sib), (4, e_x, sib), (5, e_d, sib))
        c_recvs = ((0, e_x, xpeer), (1, e_d, xpeer), (2, e_s, sib), (3, e_s + to_y, sib),
                   (4, e_s + to_x, sib), (5, e_s + to_x + to_y, sib))

        def gather_c(s, i):
            if s == 0:
                c_y(i).start()
                for k in range(1, tensor):
                    c_z(i, k, 0).start()
            if s == 1:
                c_y(i, True).wait_recv()
                for k in range(1, tensor):
                    c_z(i, k, 1).start()
            if s == 2:
                for k in range(1, tensor):
                    c_z(i, k, 0, True).wait_recv()
                for n in (0, 2):
                    c_g(i, *c_sends[n]).start()
                for k in range(1, tensor):
                    c_z(i, k, 1, True).wait_recv()
                for n in (1, 3):
                    c_g(i, *c_sends[n]).start()
            if s == 3:
                for n in (0, 1):
                    c_g(i, *c_recvs[n]).wait_recv()
                    c_g(i, *c_sends[n + 4]).start()
            if s == 4:
                for n in (2, 3, 4, 5):
                    c_g(i, *c_recvs[n]).wait_recv()

        def gather_c_drain(i):
            c_y(i).wait_send()
            for k in range(1, tensor):
                c_z(i, k, 0).wait_send()
                c_z(i, k, 1).wait_send()
            for n in range(6):
                c_g(i, *c_sends[n]).wait_send()

        def save_x(j):
            at = pl.ds(pl.multiple_of(j * CHUNK, CHUNK), CHUNK)
            return (pltpu.make_async_copy(xbuf.at[j], xs_out.at[:, at], osem.at[0, j]),
                    pltpu.make_async_copy(gbuf.at[j], gs_out.at[:, at], osem.at[1, j]))

        steps = chunks + 4 * LAG

        def gather_step(t, carry):
            for s in range(5):
                j = t - s * LAG

                @pl.when(t == s * LAG)
                def _():
                    gather_a(s, tbuf, 0, chunks)

                @pl.when(jnp.logical_and(j >= 0, j < chunks))
                def _():
                    gather_a(s, xbuf, j, j)

                    @pl.when(j % 4 != 3)
                    def _():
                        gather_c(s, j)

                    @pl.when(j % 4 == 3)
                    def _():
                        gather_a(s, gbuf, j, chunks + 1 + j // 4)

                    if s == 4:
                        for c in save_x(j):
                            c.start()
                        for n, (src, dst) in enumerate(((wg_in, wgb), (wu_in, wub), (wd_in, wdb))):
                            pltpu.make_async_copy(src.at[:, pl.ds(0, CHUNK)], dst.at[j], wsem.at[n, j]).wait()
                        gate[...] += lax.dot_general(xbuf[j], wgb[j], NT, preferred_element_type=F32)
                        up[...] += lax.dot_general(xbuf[j], wub[j], NT, preferred_element_type=F32)
                        back[...] += lax.dot_general(gbuf[j], wdb[j], NT, preferred_element_type=F32)
            return carry

        lax.fori_loop(0, steps, gather_step, 0)

        block = 32
        lane = lax.broadcasted_iota(jnp.int32, (block, tbuf.shape[2]), 1)

        def hidden_step(b, carry):
            rows = pl.ds(pl.multiple_of(b * block, block), block)
            table = tbuf[0, rows, :].astype(F32)
            placed = jnp.zeros((block, tbuf.shape[2]), F32)
            for n in range(local):
                cols = pl.ds(n * units, units)
                here = lane == e * local + n
                p = jnp.sum(jnp.where(here, table, 0.0), axis=1, keepdims=True)
                gv, uv, bv = gate[rows, cols], up[rows, cols], back[rows, cols]
                sg = jax.nn.sigmoid(gv)
                act = gv * sg
                hv = act * uv
                pb = p * bv
                dgp[rows, cols] = (pb * uv * sg * (1.0 + gv * (1.0 - sg))).astype(B16)
                dup[rows, cols] = (pb * act).astype(B16)
                hs[rows, cols] = (hv * p).astype(B16)
                placed = placed + jnp.where(here, jnp.sum(hv * bv, axis=1, keepdims=True), 0.0)
            dpb[0, rows, :] = placed.astype(B16)
            return carry

        lax.fori_loop(0, gate.shape[0] // block, hidden_step, 0)
        saves = [pltpu.make_async_copy(a, b, hsem.at[n])
                 for n, (a, b) in enumerate(((dgp, dg_out), (dup, du_out), (hs, hs_out)))]
        for c in saves:
            c.start()

        order = (3, 2, 1, 0)

        def slot(n):
            return pl.ds(n * group, group)

        def back_s(p, d, i, q, n):
            return rc(p.at[i, grp(mine[n] + to_s)], d.at[i, slot(n)], ss_s.at[q, n], ss_r.at[q, n], sib)

        def merge_s(p, d, i, q):
            for n in order:
                back_s(p, d, i, q, n).wait_recv()
                p[i, grp(mine[n]), :] = (p[i, grp(mine[n]), :].astype(F32)
                                         + d[i, slot(n), :].astype(F32)).astype(B16)

        def add(p, i, rows, cols, term):
            p[i, rows, cols] = (p[i, rows, cols].astype(F32) + term).astype(B16)

        def a_back(p, y_, x_, z_, i, q, cols, kind, n):
            if kind == 0:
                return rc(p.at[i, grp((e_y, e_d)[n]), cols], y_.at[i, slot(n)], sa_s.at[q, n], sa_r.at[q, n], ypeer)
            if kind == 1:
                return rc(p.at[i, grp(e_x), cols], x_.at[i], sa_s.at[q, 2], sa_r.at[q, 2], xpeer)
            return rc(p.at[i, row(e, zto[n]), cols], z_.at[i, pl.ds((n - 1) * tok, tok)],
                      sa_s.at[q, 2 + n], sa_r.at[q, 2 + n], zpeer[n])

        def scatter_a(s, bufs, i, q, cols, out, at):
            p, y_, x_, z_ = bufs
            args = (p, y_, x_, z_, i, q, cols)
            if s == 1:
                for n in (1, 0):
                    a_back(*args, 0, n).start()
            if s == 2:
                for n in (1, 0):
                    a_back(*args, 0, n).wait_recv()
                    add(p, i, grp((e, e_x)[n]), cols, y_[i, slot(n), :].astype(F32))
                    if n == 1:
                        a_back(*args, 1, 0).start()
            if s == 3:
                a_back(*args, 1, 0).wait_recv()
                add(p, i, grp(e), cols, x_[i].astype(F32))
                for k in range(1, tensor):
                    a_back(*args, 2, k).start()
            if s == 4:
                total = p[i, own, cols].astype(F32)
                for k in range(1, tensor):
                    a_back(*args, 2, k).wait_recv()
                    total = total + z_[i, pl.ds((k - 1) * tok, tok), :].astype(F32)
                out[:, at] = total.astype(B16)

        def scatter_a_drain(bufs, i, q, cols):
            args = (*bufs, i, q, cols)
            for n in (0, 1):
                a_back(*args, 0, n).wait_send()
            a_back(*args, 1, 0).wait_send()
            for k in range(1, tensor):
                a_back(*args, 2, k).wait_send()

        ccols = pl.ds(half, half)

        def c_back(i, kind, n, m=0):
            if kind == 0:
                return rc(pbuf.at[i, grp((e_x, e_d)[n]), ccols], cxb.at[i, slot(n)], sc_s.at[i, n], sc_r.at[i, n], xpeer)
            if kind == 1:
                at = m * others + n - 1
                return rc(pbuf.at[i, row((e, e_y)[m], zto[n]), ccols], czb.at[i, pl.ds(at * tok, tok)],
                          sc_s.at[i, 2 + at], sc_r.at[i, 2 + at], zpeer[n])
            at = 2 + 2 * others
            return rc(pbuf.at[i, row(e_y, z), ccols], cyb.at[i], sc_s.at[i, at], sc_r.at[i, at], ypeer)

        def scatter_c(s, i, out, at):
            if s == 1:
                for n in (1, 0):
                    c_back(i, 0, n).start()
            if s == 2:
                for n in (1, 0):
                    c_back(i, 0, n).wait_recv()
                    add(pbuf, i, grp((e, e_y)[n]), ccols, cxb[i, slot(n), :].astype(F32))
                    for k in range(1, tensor):
                        c_back(i, 1, k, n).start()
            if s == 3:
                for m in (1, 0):
                    total = jnp.zeros((tok, half), F32)
                    for k in range(1, tensor):
                        c_back(i, 1, k, m).wait_recv()
                        total = total + czb[i, pl.ds((m * others + k - 1) * tok, tok), :].astype(F32)
                    add(pbuf, i, row((e, e_y)[m], z), ccols, total)
                    if m == 1:
                        c_back(i, 2, 0).start()
            if s == 4:
                c_back(i, 2, 0).wait_recv()
                out[:, at] = (pbuf[i, own, ccols].astype(F32) + cyb[i].astype(F32)).astype(B16)

        def scatter_c_drain(i):
            for n in (0, 1):
                c_back(i, 0, n).wait_send()
            for m in (0, 1):
                for k in range(1, tensor):
                    c_back(i, 1, k, m).wait_send()
            c_back(i, 2, 0).wait_send()

        acols = pl.ds(0, half)
        big = (pbuf, ybuf, xb, azb)
        small = (dpb, dpy, dpx, dpz)
        all_cols = pl.ds(0, tbuf.shape[2])

        def scatter_step(t, carry):
            @pl.when(t < chunks)
            def _():
                part = jnp.dot(dgp[...], wgb[t], preferred_element_type=F32)
                part = part + jnp.dot(dup[...], wub[t], preferred_element_type=F32)
                pbuf[t] = part.astype(B16)

            for s in range(5):
                j = t - s * LAG

                @pl.when(t == s * LAG)
                def _():
                    if s == 0:
                        for n in order:
                            back_s(dpb, dps, 0, chunks, n).start()
                    if s == 1:
                        merge_s(dpb, dps, 0, chunks)
                    scatter_a(s, small, 0, chunks, all_cols, dp_out, all_cols)

                @pl.when(jnp.logical_and(j >= 0, j < chunks))
                def _():
                    if s == 0:
                        for n in order:
                            back_s(pbuf, sbuf, j, j, n).start()
                    if s == 1:
                        merge_s(pbuf, sbuf, j, j)
                    a_at = pl.ds(pl.multiple_of(j * CHUNK, CHUNK), half)
                    c_at = pl.ds(pl.multiple_of(j * CHUNK + half, half), half)
                    scatter_a(s, big, j, j, acols, dx_out, a_at)
                    scatter_c(s, j, dx_out, c_at)
            return carry

        lax.fori_loop(0, steps, scatter_step, 0)

        gather_a_drain(tbuf, 0, chunks)
        for n in order:
            back_s(dpb, dps, 0, chunks, n).wait_send()
        scatter_a_drain(small, 0, chunks, all_cols)

        def drain(j, carry):
            gather_a_drain(xbuf, j, j)

            @pl.when(j % 4 != 3)
            def _():
                gather_c_drain(j)

            @pl.when(j % 4 == 3)
            def _():
                gather_a_drain(gbuf, j, chunks + 1 + j // 4)

            for n in order:
                back_s(pbuf, sbuf, j, j, n).wait_send()
            scatter_a_drain(big, j, j, acols)
            scatter_c_drain(j)
            for c in save_x(j):
                c.wait()
            return carry

        lax.fori_loop(0, chunks, drain, 0)
        for c in saves:
            c.wait()

    return body


def fused(tokens, grad_out, table, wg, wu, wd, tensor, local, units):
    tok, width = tokens.shape
    lanes = table.shape[1]
    owners = lax.axis_size("expert")
    rows = owners * tensor * tok
    hid = local * units
    chunks = width // CHUNK
    half = CHUNK // 2
    mid = owners // 2 * tensor * tok
    two, one = 2 * tensor * tok, tensor * tok
    oth = tensor - 1
    V = pltpu.VMEM
    dma = pltpu.SemaphoreType.DMA
    scratch = [
        V((chunks, rows, CHUNK), B16), V((chunks, rows, CHUNK), B16), V((1, rows, lanes), B16),
        V((chunks, hid, CHUNK), B16), V((chunks, hid, CHUNK), B16), V((chunks, hid, CHUNK), B16),
        V((rows, hid), F32), V((rows, hid), F32), V((rows, hid), F32),
        V((rows, hid), B16), V((rows, hid), B16), V((rows, hid), B16),
        V((chunks, rows, CHUNK), B16), V((chunks, mid, CHUNK), B16),
        V((chunks, two, half), B16), V((chunks, one, half), B16), V((chunks, oth * tok, half), B16),
        V((chunks, two, half), B16), V((chunks, 2 * oth * tok, half), B16), V((chunks, tok, half), B16),
        V((1, rows, lanes), B16), V((1, mid, lanes), B16), V((1, two, lanes), B16), V((1, one, lanes), B16),
        V((1, oth * tok, lanes), B16),
        dma((2, chunks + 1)), dma((3, chunks)), dma((2, chunks)), dma((3,)),
        dma((chunks + 1 + chunks // 4, oth + 7)), dma((chunks + 1 + chunks // 4, oth + 7)),
        dma((chunks, 2 * oth + 7)), dma((chunks, 2 * oth + 7)),
        dma((chunks + 1, 4)), dma((chunks + 1, 4)),
        dma((chunks + 1, 3 + oth)), dma((chunks + 1, 3 + oth)),
        dma((chunks, 3 + 2 * oth)), dma((chunks, 3 + 2 * oth)),
    ]
    any_, vm = pl.BlockSpec(memory_space=pl.ANY), pl.BlockSpec(memory_space=pltpu.VMEM)
    sd = jax.ShapeDtypeStruct
    return pl.pallas_call(
        gather_and_send_back(tensor, tok, width, local, units),
        out_shape=(sd((tok, width), B16), sd((tok, lanes), B16), sd((rows, width), B16), sd((rows, width), B16),
                   sd((rows, hid), B16), sd((rows, hid), B16), sd((rows, hid), B16)),
        in_specs=[any_] * 6,
        out_specs=(vm, vm) + (any_,) * 5,
        scratch_shapes=scratch,
        compiler_params=pltpu.CompilerParams(collective_id=0, has_side_effects=True, vmem_limit_bytes=60 * 1024 * 1024),
        cost_estimate=pl.CostEstimate(flops=10 * rows * hid * width, transcendentals=rows * hid,
                                      bytes_accessed=6 * hid * width + 8 * rows * width),
        name="gather_and_send_back",
    )(tokens, grad_out, table, wg, wu, wd)


def with_kernel(tokens, grad_out, routes, gate_probs, w_gate, w_up, w_down):
    local, units, width = w_gate.shape
    tensor = lax.axis_size("tensor")
    ids = jnp.arange(128, dtype=jnp.int32)
    hit = routes[:, :, None] == ids[None, None, :]
    table = jnp.sum(jnp.where(hit, gate_probs[:, :, None].astype(F32), 0.0), axis=1).astype(B16)
    flat = [w.reshape(local * units, width) for w in (w_gate, w_up, w_down)]
    d_tokens, dp, xs, gs, dgp, dup, hs = fused(tokens, grad_out, table, *flat, tensor, local, units)
    tn = (((0,), (0,)), ((), ()))
    shape = (local, units, width)
    d_gate = lax.dot_general(dgp, xs, tn, preferred_element_type=F32).astype(B16).reshape(shape)
    d_up = lax.dot_general(dup, xs, tn, preferred_element_type=F32).astype(B16).reshape(shape)
    d_down = lax.dot_general(hs, gs, tn, preferred_element_type=F32).astype(B16).reshape(shape)
    d_probs = jnp.sum(jnp.where(hit, dp.astype(F32)[:, None, :], 0.0), axis=2).astype(B16)
    return (d_tokens, d_probs, d_gate, d_up, d_down)


def per_device(tokens, grad_out, routes, gate_probs, w_gate, w_up, w_down):
    local, units, width = w_gate.shape
    first = lax.axis_index("expert") * local
    mine = first + jnp.arange(local, dtype=jnp.int32)
    owners = lax.axis_size("expert")
    ids = jnp.arange(local * owners, dtype=jnp.int32)
    hit = routes[:, :, None] == ids[None, None, :]
    table = jnp.sum(jnp.where(hit, gate_probs[:, :, None].astype(jnp.float32), 0.0), axis=1)
    table = table.astype(jnp.bfloat16)
    rows_x = lax.all_gather(tokens, AXES, axis=0, tiled=True)
    rows_g = lax.all_gather(grad_out, AXES, axis=0, tiled=True)
    probs = lax.all_gather(table, AXES, axis=0, tiled=True)
    probs = lax.dynamic_slice_in_dim(probs, first, local, axis=1).astype(jnp.float32)
    count = rows_x.shape[0]
    wg = w_gate.reshape(local * units, width)
    wu = w_up.reshape(local * units, width)
    wd = w_down.reshape(local * units, width)
    nt = (((1,), (1,)), ((), ()))
    tn = (((0,), (0,)), ((), ()))
    f32 = jnp.float32
    gate = lax.dot_general(rows_x, wg, nt, preferred_element_type=f32)
    up = lax.dot_general(rows_x, wu, nt, preferred_element_type=f32)
    back = lax.dot_general(rows_g, wd, nt, preferred_element_type=f32)
    sigma = jax.nn.sigmoid(gate)
    act = gate * sigma
    hidden = act * up
    p = jnp.broadcast_to(probs[:, :, None], (count, local, units)).reshape(count, local * units)
    d_hidden = p * back
    dgp = (d_hidden * up * sigma * (1.0 + gate * (1.0 - sigma))).astype(jnp.bfloat16)
    dup = (d_hidden * act).astype(jnp.bfloat16)
    hs = (hidden * p).astype(jnp.bfloat16)
    dprob = jnp.sum((hidden * back).reshape(count, local, units), axis=2)
    part = lax.dot_general(dgp, wg, (((1,), (0,)), ((), ())), preferred_element_type=f32)
    part = part + lax.dot_general(dup, wu, (((1,), (0,)), ((), ())), preferred_element_type=f32)
    d_tokens = lax.psum_scatter(part.astype(jnp.bfloat16), AXES, scatter_dimension=0, tiled=True)
    d_gate = lax.dot_general(dgp, rows_x, tn, preferred_element_type=f32).astype(jnp.bfloat16)
    d_up = lax.dot_general(dup, rows_x, tn, preferred_element_type=f32).astype(jnp.bfloat16)
    d_down = lax.dot_general(hs, rows_g, tn, preferred_element_type=f32).astype(jnp.bfloat16)
    wide = lax.dynamic_update_slice(jnp.zeros((count, local * owners), f32), dprob, (0, first))
    mineprob = lax.psum_scatter(wide.astype(jnp.bfloat16), AXES, scatter_dimension=0, tiled=True)
    d_probs = jnp.sum(jnp.where(hit, mineprob.astype(f32)[:, None, :], 0.0), axis=2).astype(jnp.bfloat16)
    shape = (local, units, width)
    return (d_tokens, d_probs, d_gate.reshape(shape), d_up.reshape(shape), d_down.reshape(shape))


def solution(mesh):
    tok = P(AXES, None)
    wt = P("expert", "tensor", None)

    def program(tokens, grad_out, routes, gate_probs, w_gate, w_up, w_down):
        small = tokens.shape[0] <= 512 and mesh.shape["expert"] == 8 and mesh.shape["tensor"] > 1
        small = small and tokens.shape[0] // mesh.size == 16 and tokens.shape[1] % CHUNK == 0
        small = small and w_gate.shape[0] <= 128 and w_gate.shape[0] == 16
        small = small and w_gate.shape[1] // mesh.shape["tensor"] <= 384 and w_gate.shape[2] <= 4096
        return jax.shard_map(
            with_kernel if small else per_device, mesh=mesh, in_specs=(tok, tok, tok, tok, wt, wt, wt),
            out_specs=(tok, tok, wt, wt, wt), check_vma=False
        )(tokens, grad_out, routes, gate_probs, w_gate, w_up, w_down)

    return program
```
